32 devices in a mesh: tok: 16 (over z, y, core), tp: 2 (over x).
Axes of the slice: x: 2, y: 2, z: 4, core: 2. Of those that a mesh axis runs over, the one named last changes fastest.
Arguments:
- hidden_in: bfloat16 [4096, 4096], P('tok', 'tp'), may hold values from -6 to 6
- norm_gain: float32 [4096], replicated, may hold values from 0.5 to 9, as said below
- w_query: bfloat16 [4096, 4096], P(None, 'tp'), may hold values from -0.09375 to 0.09375
- w_key: bfloat16 [4096, 1024], P(None, 'tp'), may hold values from -0.09375 to 0.09375
- w_value: bfloat16 [4096, 1024], P(None, 'tp'), may hold values from -0.09375 to 0.09375
- w_out: bfloat16 [4096, 4096], P('tp'), may hold values from -0.5 to 0.5
- doc_ids: int32 [4096], replicated, may hold values from 0 to 3, never falling along the last dimension, each value on 1 to 3072 neighbouring positions
Outputs:
- hidden_out: bfloat16 [4096, 4096], P('tok', 'tp')
- joint_cov: float32 [2, 4096, 2, 4096], P(None, 'tok', None, 'tp')
The draws below stay inside these ranges and needn't reach their ends.
Inputs may be any that keep to these rules, and one draw needn't show every extreme that they name: `norm_gain`: each channel's gain is positive. `doc_ids`: document numbers never fall along the tokens; a document holds 1 to 3072 tokens.
All inputs are finite; a program needn't handle non-finite values.
Results may differ from the reference program's by a relative error of at most 0.013.
The reference program's roundings to bfloat16 on the way count: a program that leaves them out, or rounds other values in their place, can miss the bound.
Values may be sent and summed in bfloat16 or wider, within the bound.
A program may use at most 192 MiB of HBM per device.

```python
import math
import jax
import jax.numpy as jnp
import numpy as np
from jax import lax

D = 4096
HEADS = 32
KV_HEADS = 8
HS = 128
TOKENS = 4096
SEQ = 4096


def draw_norm_gain(key, part):
    return jnp.exp(jax.random.uniform(key, (D,), jnp.float32, jnp.log(0.5), jnp.log(2.0)))


def levels(key, extent, pieces, least, top_value):
    gain, own = 1.0, jax.random.fold_in(key, 6)
    for dim, blocks in pieces:
        heights = jnp.exp(jax.random.uniform(jax.random.fold_in(own, dim), (blocks,), jnp.float32, least / len(pieces), top_value / len(pieces)))
        gain = gain * jnp.repeat(heights, extent[dim] // blocks).reshape([-1 if axis == dim else 1 for axis in range(len(extent))])
    return gain


def length_profile(count, total, limit, lean):
    portions = [(1 << 20) // math.isqrt(grade ** lean) + 1 for grade in range(2, count + 1)]
    spare, given = total - limit - (count - 1), [1] * (count - 1)
    while spare > 0:
        candidates = [i for i in range(count - 1) if given[i] < limit]
        mass, budget = sum([portions[i] for i in candidates]), spare
        for i in candidates:
            addition = min(limit - given[i], max(1, budget * portions[i] // mass), spare)
            given[i] = given[i] + addition
            spare = spare - addition
    return np.array([limit] + given)


def uneven_parts(rng, count, total, bound, skew):
    if count == 2:
        one = jax.random.randint(rng, (), max(1, total - bound), min(bound, total - 1) + 1)
        return jnp.stack([one, total - one])
    lengths = jnp.asarray(length_profile(count, total, bound, skew), jnp.int32)
    pairs = (count - 1) // 2
    source_of, taker = lengths[1:1 + 2 * pairs:2], lengths[2:2 + 2 * pairs:2]
    margin = jnp.minimum(source_of - 1, bound - taker)
    moved = jax.random.randint(jax.random.fold_in(rng, 1), (pairs,), 0, 1 << 20) % (margin + 1)
    lengths = lengths.at[1:1 + 2 * pairs:2].set(source_of - moved).at[2:2 + 2 * pairs:2].set(taker + moved)
    return lengths[jax.random.permutation(jax.random.fold_in(rng, 2), count)]


def scatter_about(rng, extent, width, bound, shards=(), held_as=jnp.bfloat16):
    array = width * jax.random.normal(rng, extent, jnp.float32)
    if shards:
        array = array * levels(rng, extent, shards, -0.22, 0.18)
    return jnp.clip(array, -bound, bound).astype(held_as)


def setup_inputs(seed: int = 0) -> dict:
    key_list = jax.random.split(jax.random.key(seed), 8)
    return {
        "hidden_in": scatter_about(key_list[0], (TOKENS, D), 1.0, 6.0, ((0, 16), (1, 2))),
        "norm_gain": draw_norm_gain(jax.random.fold_in(key_list[7], 71), 0),
        "w_query": scatter_about(key_list[2], (D, HEADS * HS), D ** -0.5, 0.09375, ((1, 2),)),
        "w_key": scatter_about(key_list[3], (D, KV_HEADS * HS), D ** -0.5, 0.09375, ((1, 2),)),
        "w_value": scatter_about(key_list[4], (D, KV_HEADS * HS), D ** -0.5, 0.09375, ((1, 2),)),
        "w_out": scatter_about(key_list[5], (HEADS * HS, D), HS ** -0.5, 0.5, ((0, 2),)),
        "doc_ids": jnp.searchsorted(jnp.cumsum(uneven_parts(key_list[6], 4, TOKENS, 3 * SEQ // 4, 2)), jnp.arange(TOKENS), side="right").astype(jnp.int32),
    }


epsilon = 1e-05
rope_base = 500000.0

def rotate(vectors, positions):
    half_dim = vectors.shape[-1] // 2
    inv_freq = rope_base ** (-(jnp.arange(half_dim, dtype=jnp.float32) * 2.0) / vectors.shape[-1])
    angles = positions.astype(jnp.float32)[:, None] * inv_freq[None, :]
    cosine = jnp.cos(angles)[:, None, :]
    sine_part = jnp.sin(angles)[:, None, :]
    first_half = vectors[..., :half_dim]
    second_half = vectors[..., half_dim:]
    return jnp.concatenate([first_half * cosine - second_half * sine_part, second_half * cosine + first_half * sine_part], axis=-1)

def reference(hidden_in, norm_gain, w_query, w_key, w_value, w_out, doc_ids):
    widened = hidden_in.astype(jnp.float32)
    factor = lax.rsqrt(lax.optimization_barrier(jnp.mean(widened * widened, axis=1, keepdims=True)) + epsilon)
    normed = (widened * factor * norm_gain[None, :]).astype(jnp.bfloat16)
    groups = HEADS // KV_HEADS
    positions = jnp.arange(TOKENS, dtype=jnp.int32)
    queries = rotate(jnp.dot(normed, w_query, preferred_element_type=jnp.float32).reshape(TOKENS, HEADS, HS), positions % SEQ)
    queries = queries.astype(jnp.bfloat16).reshape(TOKENS, KV_HEADS, groups, HS)
    key_rows = rotate(jnp.dot(normed, w_key, preferred_element_type=jnp.float32).reshape(TOKENS, KV_HEADS, HS), positions % SEQ).astype(jnp.bfloat16)
    value_rows = jnp.dot(normed, w_value, preferred_element_type=jnp.float32).astype(jnp.bfloat16).reshape(TOKENS, KV_HEADS, HS)
    block_size = SEQ // 16
    key_wide = key_rows.astype(jnp.float32)
    value_wide = value_rows.astype(jnp.float32)

    def attend(number):
        anchor = (number * block_size).astype(jnp.int32)
        seq_anchor = (anchor // SEQ * SEQ).astype(jnp.int32)
        query_part = lax.dynamic_slice_in_dim(queries, anchor, block_size, 0).astype(jnp.float32)
        query_pos = anchor + jnp.arange(block_size, dtype=jnp.int32)
        query_doc = lax.dynamic_slice_in_dim(doc_ids, anchor, block_size, 0)
        key_pos = seq_anchor + jnp.arange(SEQ, dtype=jnp.int32)
        key_doc = lax.dynamic_slice_in_dim(doc_ids, seq_anchor, SEQ, 0)
        key_part = lax.dynamic_slice_in_dim(key_wide, seq_anchor, SEQ, 0)
        value_part = lax.dynamic_slice_in_dim(value_wide, seq_anchor, SEQ, 0)
        allowed = (query_doc[:, None] == key_doc[None, :]) & (key_pos[None, :] <= query_pos[:, None])
        scores = jnp.einsum('qhgd,khd->hgqk', query_part, key_part) * HS ** (-0.5)
        scores = jnp.where(allowed[None, None], scores, -jnp.inf)
        row_max = lax.optimization_barrier(jnp.max(scores, axis=-1, keepdims=True))
        weights = jnp.exp(scores - row_max)
        weight_sum = lax.optimization_barrier(jnp.sum(weights, axis=-1, keepdims=True))
        rounded = lax.optimization_barrier(weights.astype(jnp.bfloat16)).astype(jnp.float32)
        blended = jnp.einsum('hgqk,khd->hgqd', rounded, value_part) / weight_sum
        return jnp.transpose(blended, (2, 0, 1, 3)).astype(jnp.bfloat16)
    attended = lax.map(attend, jnp.arange(TOKENS // block_size, dtype=jnp.int32)).reshape(TOKENS, HEADS * HS)
    layer_sum = jnp.dot(attended, w_out, preferred_element_type=jnp.float32)
    hidden_out = (widened + layer_sum).astype(jnp.bfloat16)
    joint_rows = jnp.stack([hidden_in, hidden_out], axis=1).reshape(TOKENS, 2 * D)
    gram_block = lax.dot_general(joint_rows, joint_rows, (((0,), (0,)), ((), ())), preferred_element_type=jnp.float32)
    means = lax.optimization_barrier(jnp.sum(joint_rows, axis=0, dtype=jnp.float32)) / TOKENS
    joint_cov = (gram_block / TOKENS - means[:, None] * means[None, :]).reshape(2, D, 2, D)
    return (hidden_out, joint_cov)
```

```python
import functools
import math

import jax
import jax.numpy as jnp
from jax import lax
from jax.experimental import pallas as pl
from jax.experimental.pallas import tpu as pltpu
from jax.sharding import PartitionSpec as P

HS = 128
epsilon = 1e-05
rope_base = 500000.0
VMEM_LIMIT = 60 * 1024 * 1024


def rotate(vectors, positions):
    half_dim = vectors.shape[-1] // 2
    inv_freq = rope_base ** (-(jnp.arange(half_dim, dtype=jnp.float32) * 2.0) / vectors.shape[-1])
    angles = positions.astype(jnp.float32)[:, None] * inv_freq[None, :]
    cosine = jnp.cos(angles)[:, None, :]
    sine_part = jnp.sin(angles)[:, None, :]
    first_half = vectors[..., :half_dim]
    second_half = vectors[..., half_dim:]
    return jnp.concatenate(
        [
            first_half * cosine - second_half * sine_part,
            second_half * cosine + first_half * sine_part,
        ],
        axis=-1,
    )


def attend_kernel(groups, block, bounds, q_ref, k_ref, v_ref, lo_ref, out_ref, s_ref, m_ref, l_ref, acc_ref):
    rows = q_ref.shape[0]
    first_row = bounds[0]
    scale = HS ** (-0.5) * math.log2(math.e)
    start = bounds[1] // block
    stop = (first_row + rows + block - 1) // block
    lanes = 128
    m_ref[...] = jnp.full_like(m_ref, -jnp.inf)
    l_ref[...] = jnp.zeros_like(l_ref)
    acc_ref[...] = jnp.zeros_like(acc_ref)

    @pl.loop(start, stop)
    def _(step):
        first_key = pl.multiple_of(step * block, block)
        keys = k_ref[pl.ds(first_key, block), :]
        key_pos = first_key + lax.broadcasted_iota(jnp.int32, (rows, block), 1)
        query_pos = first_row + lax.broadcasted_iota(jnp.int32, (rows, block), 0)
        allowed = (key_pos >= lo_ref[:, :1]) & (key_pos <= query_pos)
        for head in range(groups):
            part = pl.ds(head * rows, rows)
            s = lax.dot_general(
                q_ref[:, head * HS:(head + 1) * HS], keys,
                (((1,), (1,)), ((), ())), preferred_element_type=jnp.float32,
            ) * scale
            s = jnp.where(allowed, s, -jnp.inf)
            s_ref[step, part, :] = s
            top = m_ref[part, :]
            for piece in range(block // lanes):
                top = jnp.maximum(top, s[:, piece * lanes:(piece + 1) * lanes])
            m_ref[part, :] = top

    m_ref[...] = jnp.broadcast_to(jnp.max(m_ref[...], axis=-1, keepdims=True), m_ref.shape)

    @pl.loop(start, stop)
    def _(step):
        first_key = pl.multiple_of(step * block, block)
        values = v_ref[pl.ds(first_key, block), :]
        for head in range(groups):
            part = pl.ds(head * rows, rows)
            weights = jnp.exp2(s_ref[step, part, :] - m_ref[part, :1])
            total = l_ref[part, :]
            for piece in range(block // lanes):
                total = total + weights[:, piece * lanes:(piece + 1) * lanes]
            l_ref[part, :] = total
            acc_ref[part, :] += jnp.dot(
                weights.astype(jnp.bfloat16), values, preferred_element_type=jnp.float32
            )

    for head in range(groups):
        part = pl.ds(head * rows, rows)
        weight_sum = jnp.sum(l_ref[part, :], axis=-1, keepdims=True)
        out_ref[:, head * HS:(head + 1) * HS] = (acc_ref[part, :] / weight_sum).astype(out_ref.dtype)


def attend(queries, kv_rows, lo, bounds, kv_heads):
    rows, width = queries.shape
    all_rows = kv_rows.shape[0]
    groups = width // (kv_heads * HS)
    block = min(512, all_rows)
    wide = groups * HS
    return pl.pallas_call(
        functools.partial(attend_kernel, groups, block),
        out_shape=jax.ShapeDtypeStruct((rows, width), jnp.bfloat16),
        grid_spec=pltpu.PrefetchScalarGridSpec(
            num_scalar_prefetch=1,
            grid=(kv_heads,),
            in_specs=[
                pl.BlockSpec((rows, wide), lambda g, b: (0, g)),
                pl.BlockSpec((all_rows, HS), lambda g, b: (0, g)),
                pl.BlockSpec((all_rows, HS), lambda g, b: (0, kv_heads + g)),
                pl.BlockSpec((rows, 128), lambda g, b: (0, 0)),
            ],
            out_specs=pl.BlockSpec((rows, wide), lambda g, b: (0, g)),
            scratch_shapes=[
                pltpu.VMEM((all_rows // block, groups * rows, block), jnp.float32),
                pltpu.VMEM((groups * rows, 128), jnp.float32),
                pltpu.VMEM((groups * rows, 128), jnp.float32),
                pltpu.VMEM((groups * rows, HS), jnp.float32),
            ],
        ),
        compiler_params=pltpu.CompilerParams(
            dimension_semantics=("arbitrary",), vmem_limit_bytes=VMEM_LIMIT
        ),
        cost_estimate=pl.CostEstimate(
            flops=4 * rows * all_rows * width,
            bytes_accessed=2 * all_rows * kv_heads * HS * 2 + 4 * rows * width,
            transcendentals=rows * all_rows * width // HS,
        ),
        name="attend",
    )(bounds, queries, kv_rows, kv_rows, lo)


def gram_kernel(rin_ref, rout_ref, cin_ref, cout_ref, out_ref, rt_ref, mean_ref):
    all_rows, row_width = rin_ref.shape

    @pl.when(pl.program_id(0) == 0)
    def _():
        ones = jnp.ones((all_rows, 128), jnp.bfloat16)
        for source, ref in enumerate((rin_ref, rout_ref)):
            part = pl.ds(source * row_width, row_width)
            rt_ref[part, :] = ref[...].T
            mean_ref[part, :] = (
                jnp.dot(rt_ref[part, :], ones, preferred_element_type=jnp.float32) / all_rows
            )

    ones = jnp.ones((8, all_rows), jnp.bfloat16)
    for source, ref in enumerate((cin_ref, cout_ref)):
        cols = ref[...]
        col_mean = jnp.dot(ones, cols, preferred_element_type=jnp.float32)[:1] / all_rows
        gram = jnp.dot(rt_ref[...], cols, preferred_element_type=jnp.float32)
        cov = gram / all_rows - mean_ref[:, :1] * col_mean
        for row_source in range(2):
            out_ref[row_source, :, source, :] = cov[row_source * row_width:(row_source + 1) * row_width]


def joint_gram(rin, rout, cin, cout):
    all_rows, row_width = rin.shape
    col_width = cin.shape[1]
    tile = min(256, col_width)
    whole = pl.BlockSpec((all_rows, row_width), lambda j: (0, 0), pipeline_mode=pl.Buffered(1))
    strip = pl.BlockSpec((all_rows, tile), lambda j: (0, j))
    return pl.pallas_call(
        gram_kernel,
        out_shape=jax.ShapeDtypeStruct((2, row_width, 2, col_width), jnp.float32),
        grid=(col_width // tile,),
        in_specs=[whole, whole, strip, strip],
        out_specs=pl.BlockSpec((2, row_width, 2, tile), lambda j: (0, 0, 0, j)),
        scratch_shapes=[
            pltpu.VMEM((2 * row_width, all_rows), jnp.bfloat16),
            pltpu.VMEM((2 * row_width, 128), jnp.float32),
        ],
        compiler_params=pltpu.CompilerParams(
            dimension_semantics=("arbitrary",), vmem_limit_bytes=VMEM_LIMIT
        ),
        cost_estimate=pl.CostEstimate(
            flops=8 * all_rows * row_width * col_width,
            bytes_accessed=4 * all_rows * (row_width + col_width) + 16 * row_width * col_width,
            transcendentals=0,
        ),
        name="joint_gram",
    )(rin, rout, cin, cout)


def both_sides(block):
    if lax.axis_size("tp") != 2:
        return lax.all_gather(block, "tp", axis=1, tiled=True)
    other = lax.ppermute(block, "tp", ((0, 1), (1, 0)))
    first = lax.axis_index("tp") == 0
    return jnp.concatenate([jnp.where(first, block, other), jnp.where(first, other, block)], axis=1)


def on_device(hidden_in, norm_gain, w_query, w_key, w_value, w_out, doc_ids):
    tok_rows, col_width = hidden_in.shape
    tok_count = lax.axis_size("tok")
    tp_count = lax.axis_size("tp")
    tok_index = lax.axis_index("tok")
    all_rows = tok_rows * tok_count
    full_in = both_sides(hidden_in)
    widened = full_in.astype(jnp.float32)
    factor = lax.rsqrt(jnp.mean(widened * widened, axis=1, keepdims=True) + epsilon)
    normed = (widened * factor * norm_gain[None, :]).astype(jnp.bfloat16)
    kv_heads = w_key.shape[1] // HS
    groups = w_query.shape[1] // w_key.shape[1]
    first_row = tok_index * tok_rows
    positions = first_row + jnp.arange(tok_rows, dtype=jnp.int32)
    key_local = rotate(
        jnp.dot(normed, w_key, preferred_element_type=jnp.float32).reshape(tok_rows, kv_heads, HS),
        positions % all_rows,
    )
    key_local = key_local.astype(jnp.bfloat16).reshape(tok_rows, kv_heads * HS)
    value_local = jnp.dot(normed, w_value, preferred_element_type=jnp.float32).astype(jnp.bfloat16)
    kv_local = jnp.concatenate([key_local, value_local], axis=1)
    kv_rows = lax.all_gather(kv_local, "tok", axis=0, tiled=True)
    late_in, full_late, kv_rows = lax.optimization_barrier((hidden_in, full_in, kv_rows))
    cols_in = lax.all_gather(late_in, "tok", axis=0, tiled=True)
    rows_in = lax.all_to_all(full_in, "tok", 1, 0, tiled=True)
    queries = rotate(
        jnp.dot(normed, w_query, preferred_element_type=jnp.float32).reshape(
            tok_rows, kv_heads * groups, HS
        ),
        positions % all_rows,
    )
    queries = queries.astype(jnp.bfloat16).reshape(tok_rows, kv_heads * groups * HS)
    query_doc = lax.dynamic_slice_in_dim(doc_ids, first_row, tok_rows, 0)
    lo = jnp.sum((doc_ids[None, :] < query_doc[:, None]).astype(jnp.int32), axis=1)
    bounds = jnp.stack([first_row.astype(jnp.int32), lo[0]])
    attended = attend(queries, kv_rows, jnp.broadcast_to(lo[:, None], (tok_rows, 128)), bounds, kv_heads)
    partial_out = jnp.dot(attended, w_out, preferred_element_type=jnp.float32)
    if tp_count == 2:
        first = lax.axis_index("tp") == 0
        low, high = partial_out[:, :col_width], partial_out[:, col_width:]
        sent = jnp.where(first, high, low).astype(jnp.bfloat16)
        arrived = lax.ppermute(sent, "tp", ((0, 1), (1, 0)))
        summed = jnp.where(first, low, high) + arrived.astype(jnp.float32)
    else:
        summed = lax.psum_scatter(partial_out, "tp", scatter_dimension=1, tiled=True)
    hidden_out = (hidden_in.astype(jnp.float32) + summed).astype(jnp.bfloat16)
    cols_out = lax.all_gather(hidden_out, "tok", axis=0, tiled=True)
    rows_out = lax.all_to_all(both_sides(hidden_out), "tok", 1, 0, tiled=True)
    return (hidden_out, joint_gram(rows_in, rows_out, cols_in, cols_out))


def solution(mesh):
    return jax.shard_map(
        on_device,
        mesh=mesh,
        in_specs=(
            P("tok", "tp"),
            P(),
            P(None, "tp"),
            P(None, "tp"),
            P(None, "tp"),
            P("tp", None),
            P(),
        ),
        out_specs=(P("tok", "tp"), P(None, "tok", None, "tp")),
        check_vma=False,
    )
```

```python
import functools
import math

import jax
import jax.numpy as jnp
from jax import lax
from jax.experimental import pallas as pl
from jax.experimental.pallas import tpu as pltpu
from jax.sharding import PartitionSpec as P

HS = 128
epsilon = 1e-05
rope_base = 500000.0
VMEM_LIMIT = 60 * 1024 * 1024


def rotate(vectors, positions):
    half_dim = vectors.shape[-1] // 2
    inv_freq = rope_base ** (-(jnp.arange(half_dim, dtype=jnp.float32) * 2.0) / vectors.shape[-1])
    angles = positions.astype(jnp.float32)[:, None] * inv_freq[None, :]
    cosine = jnp.cos(angles)[:, None, :]
    sine_part = jnp.sin(angles)[:, None, :]
    first_half = vectors[..., :half_dim]
    second_half = vectors[..., half_dim:]
    return jnp.concatenate(
        [
            first_half * cosine - second_half * sine_part,
            second_half * cosine + first_half * sine_part,
        ],
        axis=-1,
    )


def attend_kernel(groups, block, bounds, q_ref, k_ref, v_ref, lo_ref, out_ref, s_ref, m_ref, l_ref, acc_ref):
    rows = q_ref.shape[0]
    first_row = bounds[0]
    scale = HS ** (-0.5) * math.log2(math.e)
    start = bounds[1] // block
    stop = (first_row + rows + block - 1) // block
    lanes = 128
    m_ref[...] = jnp.full_like(m_ref, -jnp.inf)
    l_ref[...] = jnp.zeros_like(l_ref)
    acc_ref[...] = jnp.zeros_like(acc_ref)

    @pl.loop(start, stop)
    def _(step):
        first_key = pl.multiple_of(step * block, block)
        keys = k_ref[pl.ds(first_key, block), :]
        key_pos = first_key + lax.broadcasted_iota(jnp.int32, (rows, block), 1)
        query_pos = first_row + lax.broadcasted_iota(jnp.int32, (rows, block), 0)
        allowed = (key_pos >= lo_ref[:, :1]) & (key_pos <= query_pos)
        for head in range(groups):
            part = pl.ds(head * rows, rows)
            s = lax.dot_general(
                q_ref[:, head * HS:(head + 1) * HS], keys,
                (((1,), (1,)), ((), ())), preferred_element_type=jnp.float32,
            ) * scale
            s = jnp.where(allowed, s, -jnp.inf)
            s_ref[step, part, :] = s
            top = m_ref[part, :]
            for piece in range(block // lanes):
                top = jnp.maximum(top, s[:, piece * lanes:(piece + 1) * lanes])
            m_ref[part, :] = top

    m_ref[...] = jnp.broadcast_to(jnp.max(m_ref[...], axis=-1, keepdims=True), m_ref.shape)

    @pl.loop(start, stop)
    def _(step):
        first_key = pl.multiple_of(step * block, block)
        values = v_ref[pl.ds(first_key, block), :]
        for head in range(groups):
            part = pl.ds(head * rows, rows)
            weights = jnp.exp2(s_ref[step, part, :] - m_ref[part, :1])
            total = l_ref[part, :]
            for piece in range(block // lanes):
                total = total + weights[:, piece * lanes:(piece + 1) * lanes]
            l_ref[part, :] = total
            acc_ref[part, :] += jnp.dot(
                weights.astype(jnp.bfloat16), values, preferred_element_type=jnp.float32
            )

    for head in range(groups):
        part = pl.ds(head * rows, rows)
        weight_sum = jnp.sum(l_ref[part, :], axis=-1, keepdims=True)
        out_ref[:, head * HS:(head + 1) * HS] = (acc_ref[part, :] / weight_sum).astype(out_ref.dtype)


def attend(queries, kv_rows, lo, bounds, kv_heads):
    rows, width = queries.shape
    all_rows = kv_rows.shape[1]
    groups = width // (kv_heads * HS)
    block = min(512, all_rows)
    wide = groups * HS
    return pl.pallas_call(
        functools.partial(attend_kernel, groups, block),
        out_shape=jax.ShapeDtypeStruct((rows, width), jnp.bfloat16),
        grid_spec=pltpu.PrefetchScalarGridSpec(
            num_scalar_prefetch=1,
            grid=(kv_heads,),
            in_specs=[
                pl.BlockSpec((rows, wide), lambda g, b: (0, g)),
                pl.BlockSpec((None, all_rows, HS), lambda g, b: (0, 0, g)),
                pl.BlockSpec((None, all_rows, HS), lambda g, b: (1, 0, g)),
                pl.BlockSpec((rows, 128), lambda g, b: (0, 0)),
            ],
            out_specs=pl.BlockSpec((rows, wide), lambda g, b: (0, g)),
            scratch_shapes=[
                pltpu.VMEM((all_rows // block, groups * rows, block), jnp.float32),
                pltpu.VMEM((groups * rows, 128), jnp.float32),
                pltpu.VMEM((groups * rows, 128), jnp.float32),
                pltpu.VMEM((groups * rows, HS), jnp.float32),
            ],
        ),
        compiler_params=pltpu.CompilerParams(
            dimension_semantics=("arbitrary",), vmem_limit_bytes=VMEM_LIMIT
        ),
        cost_estimate=pl.CostEstimate(
            flops=4 * rows * all_rows * width,
            bytes_accessed=2 * all_rows * kv_heads * HS * 2 + 4 * rows * width,
            transcendentals=rows * all_rows * width // HS,
        ),
        name="attend",
    )(bounds, queries, kv_rows, kv_rows, lo)


def gram_kernel(rin_ref, rout_ref, cin_ref, cout_ref, out_ref, rt_ref, mean_ref):
    all_rows, row_width = rin_ref.shape

    @pl.when(pl.program_id(0) == 0)
    def _():
        ones = jnp.ones((all_rows, 128), jnp.bfloat16)
        for source, ref in enumerate((rin_ref, rout_ref)):
            part = pl.ds(source * row_width, row_width)
            rt_ref[part, :] = ref[...].T
            mean_ref[part, :] = (
                jnp.dot(rt_ref[part, :], ones, preferred_element_type=jnp.float32) / all_rows
            )

    ones = jnp.ones((8, all_rows), jnp.bfloat16)
    for source, ref in enumerate((cin_ref, cout_ref)):
        cols = ref[...]
        col_mean = jnp.dot(ones, cols, preferred_element_type=jnp.float32)[:1] / all_rows
        gram = jnp.dot(rt_ref[...], cols, preferred_element_type=jnp.float32)
        cov = gram / all_rows - mean_ref[:, :1] * col_mean
        for row_source in range(2):
            out_ref[row_source, :, source, :] = cov[row_source * row_width:(row_source + 1) * row_width]


def joint_gram(rin, rout, cin, cout):
    all_rows, row_width = rin.shape
    half = cin.shape[2]
    col_width = 2 * half
    tile = min(256, half)
    strips = half // tile
    whole = pl.BlockSpec((all_rows, row_width), lambda j: (0, 0), pipeline_mode=pl.Buffered(1))
    strip = pl.BlockSpec((None, all_rows, tile), lambda j: (j // strips, 0, j % strips))
    return pl.pallas_call(
        gram_kernel,
        out_shape=jax.ShapeDtypeStruct((2, row_width, 2, col_width), jnp.float32),
        grid=(col_width // tile,),
        in_specs=[whole, whole, strip, strip],
        out_specs=pl.BlockSpec((2, row_width, 2, tile), lambda j: (0, 0, 0, j)),
        scratch_shapes=[
            pltpu.VMEM((2 * row_width, all_rows), jnp.bfloat16),
            pltpu.VMEM((2 * row_width, 128), jnp.float32),
        ],
        compiler_params=pltpu.CompilerParams(
            dimension_semantics=("arbitrary",), vmem_limit_bytes=VMEM_LIMIT
        ),
        cost_estimate=pl.CostEstimate(
            flops=8 * all_rows * row_width * col_width,
            bytes_accessed=4 * all_rows * (row_width + col_width) + 16 * row_width * col_width,
            transcendentals=0,
        ),
        name="joint_gram",
    )(rin, rout, cin, cout)


def both_sides(block):
    if lax.axis_size("tp") != 2:
        return lax.all_gather(block, "tp", axis=1, tiled=True)
    other = lax.ppermute(block, "tp", ((0, 1), (1, 0)))
    first = lax.axis_index("tp") == 0
    return jnp.concatenate([jnp.where(first, block, other), jnp.where(first, other, block)], axis=1)


def ring_kernel(chips, share, x_ref, *refs):
    if share:
        out_ref, side_ref, send, recv, psend, precv, local, ssend, srecv = refs
    else:
        out_ref, send, recv, psend, precv, local = refs
    mesh_id = pl.DeviceIdType.MESH
    rows = x_ref.shape[1]
    me, tp = lax.axis_index("tok"), lax.axis_index("tp")
    count = 2 * chips
    core, chip = me % 2, me // 2
    depth = chips // 2
    spot = jnp.where(chip % 2 == 0, chip // 2, chips - 1 - chip // 2)

    def device(place):
        place = (place + 2 * chips) % chips
        return jnp.where(place < depth, place * 4, (chips - 1 - place) * 4 + 2) + core

    partner = me + 1 - 2 * core
    ways = (device(spot + 1), device(spot - 1))
    barrier = pltpu.get_barrier_semaphore()
    for peer in (*ways, partner):
        pl.semaphore_signal(barrier, inc=1, device_id={"tok": peer}, device_id_type=mesh_id)
    if share:
        for peer in range(count):
            pl.semaphore_signal(barrier, inc=1, device_id={"tok": peer, "tp": 1 - tp}, device_id_type=mesh_id)
    pl.semaphore_wait(barrier, 3 + (count if share else 0))

    def block(way, origin):
        return out_ref.at[way, pl.ds(pl.multiple_of(origin * rows, rows), rows), :]

    pending = []

    def step_copies(step, way):
        origin = device(spot - step if way == 0 else spot + step)
        source = x_ref.at[way] if step == 0 else block(way, origin)
        ring = None
        if step < chips - 1:
            ring = pltpu.make_async_remote_copy(
                src_ref=source, dst_ref=block(way, origin), send_sem=send.at[way, step],
                recv_sem=recv.at[way, step], device_id={"tok": ways[way]}, device_id_type=mesh_id,
            )
            ring.start()
        beside = pltpu.make_async_remote_copy(
            src_ref=source, dst_ref=block(way, origin), send_sem=psend.at[way, step],
            recv_sem=precv.at[way, step], device_id={"tok": partner}, device_id_type=mesh_id,
        )
        beside.start()
        pending.append((ring, beside))
        return ring

    rings = [step_copies(0, way) for way in range(2)]
    own = [pltpu.make_async_copy(x_ref.at[way], block(way, me), local.at[way]) for way in range(2)]
    for copy in own:
        copy.start()
    sides = []
    if share:
        width = side_ref.shape[1]
        per_half = x_ref.shape[2] // width
        for j in range(count // 2):
            copy = pltpu.make_async_remote_copy(
                src_ref=x_ref.at[j // per_half, :, pl.ds(j % per_half * width, width)],
                dst_ref=side_ref.at[pl.ds(pl.multiple_of(me * rows, rows), rows), :],
                send_sem=ssend.at[j], recv_sem=srecv.at[me],
                device_id={"tok": tp * (count // 2) + j, "tp": 1 - tp}, device_id_type=mesh_id,
            )
            copy.start()
            sides.append(copy)
    for step in range(1, chips):
        for way in range(2):
            rings[way].wait_recv()
            rings[way] = step_copies(step, way)
    for ring, beside in pending:
        if ring is not None:
            ring.wait_send()
        beside.wait_send()
        beside.wait_recv()
    for copy in own:
        copy.wait()
    for copy in sides:
        copy.wait_send()
    if share:
        @pl.when(me // (count // 2) != tp)
        def _():
            for sender in range(count):
                landed = side_ref.at[pl.ds(sender * rows, rows), :]
                pltpu.make_async_remote_copy(
                    src_ref=landed, dst_ref=landed, send_sem=ssend.at[0], recv_sem=srecv.at[sender],
                    device_id={"tok": sender, "tp": 1 - tp}, device_id_type=mesh_id,
                ).wait_recv()


def ring_gather(halves, share, call_id):
    _, rows, width = halves.shape
    count = lax.axis_size("tok")
    chips = count // 2
    out_shape = [jax.ShapeDtypeStruct((2, rows * count, width), halves.dtype)]
    dma = pltpu.SemaphoreType.DMA
    scratch = [dma((2, chips))] * 4 + [dma((2,))]
    if share:
        out_shape.append(jax.ShapeDtypeStruct((rows * count, 4 * width // count), halves.dtype))
        scratch += [dma((count // 2,)), dma((count,))]
    return pl.pallas_call(
        functools.partial(ring_kernel, chips, share),
        out_shape=out_shape,
        in_specs=[pl.BlockSpec(memory_space=pltpu.VMEM)],
        out_specs=[pl.BlockSpec(memory_space=pl.ANY)] * len(out_shape),
        scratch_shapes=scratch,
        compiler_params=pltpu.CompilerParams(
            collective_id=call_id, has_side_effects=True, vmem_limit_bytes=8 * 1024 * 1024
        ),
        cost_estimate=pl.CostEstimate(
            flops=40_000_000_000, bytes_accessed=2 * halves.size * count * 2, transcendentals=0
        ),
        name="ring_share" if share else "ring",
    )(halves)


def gather_halves(block):
    rows, width = block.shape
    halves = jnp.stack([block[:, : width // 2], block[:, width // 2 :]])
    return lax.all_gather(halves, "tok", axis=1, tiled=True)


def row_features(columns, arrived):
    _, all_rows, half = columns.shape
    row_width = 2 * half * lax.axis_size("tp") // lax.axis_size("tok")
    first = lax.axis_index("tok") * row_width
    offset, owner = first % (2 * half), first // (2 * half)
    mine = lax.dynamic_slice(columns, (offset // half, 0, offset % half), (1, all_rows, row_width))[0]
    owned = lax.axis_index("tp") == owner
    if arrived is None:
        return lax.psum(jnp.where(owned, mine, jnp.zeros_like(mine)), "tp")
    return jnp.where(owned, mine, arrived)


def on_device(hidden_in, norm_gain, w_query, w_key, w_value, w_out, doc_ids):
    tok_rows, col_width = hidden_in.shape
    tok_count = lax.axis_size("tok")
    tp_count = lax.axis_size("tp")
    tok_index = lax.axis_index("tok")
    all_rows = tok_rows * tok_count
    full_in = both_sides(hidden_in)
    widened = full_in.astype(jnp.float32)
    factor = lax.rsqrt(jnp.mean(widened * widened, axis=1, keepdims=True) + epsilon)
    normed = (widened * factor * norm_gain[None, :]).astype(jnp.bfloat16)
    kv_heads = w_key.shape[1] // HS
    groups = w_query.shape[1] // w_key.shape[1]
    first_row = tok_index * tok_rows
    positions = first_row + jnp.arange(tok_rows, dtype=jnp.int32)
    key_local = rotate(
        jnp.dot(normed, w_key, preferred_element_type=jnp.float32).reshape(tok_rows, kv_heads, HS),
        positions % all_rows,
    )
    key_local = key_local.astype(jnp.bfloat16).reshape(tok_rows, kv_heads * HS)
    value_local = jnp.dot(normed, w_value, preferred_element_type=jnp.float32).astype(jnp.bfloat16)
    (kv_rows,) = ring_gather(jnp.stack([key_local, value_local]), False, 0)
    cols_in = gather_halves(hidden_in)
    rows_in = lax.all_to_all(full_in, "tok", 1, 0, tiled=True)
    queries = rotate(
        jnp.dot(normed, w_query, preferred_element_type=jnp.float32).reshape(
            tok_rows, kv_heads * groups, HS
        ),
        positions % all_rows,
    )
    queries = queries.astype(jnp.bfloat16).reshape(tok_rows, kv_heads * groups * HS)
    query_doc = lax.dynamic_slice_in_dim(doc_ids, first_row, tok_rows, 0)
    lo = jnp.sum((doc_ids[None, :] < query_doc[:, None]).astype(jnp.int32), axis=1)
    bounds = jnp.stack([first_row.astype(jnp.int32), lo[0]])
    attended = attend(queries, kv_rows, jnp.broadcast_to(lo[:, None], (tok_rows, 128)), bounds, kv_heads)
    partial_out = jnp.dot(attended, w_out, preferred_element_type=jnp.float32)
    if tp_count == 2:
        first = lax.axis_index("tp") == 0
        low, high = partial_out[:, :col_width], partial_out[:, col_width:]
        sent = jnp.where(first, high, low).astype(jnp.bfloat16)
        arrived = lax.ppermute(sent, "tp", ((0, 1), (1, 0)))
        summed = jnp.where(first, low, high) + arrived.astype(jnp.float32)
    else:
        summed = lax.psum_scatter(partial_out, "tp", scatter_dimension=1, tiled=True)
    hidden_out = (hidden_in.astype(jnp.float32) + summed).astype(jnp.bfloat16)
    halves = jnp.stack([hidden_out[:, : col_width // 2], hidden_out[:, col_width // 2 :]])
    if tp_count == 2:
        cols_out, arrived_rows = ring_gather(halves, True, 1)
        rows_out = row_features(cols_out, arrived_rows)
    else:
        (cols_out,) = ring_gather(halves, False, 1)
        rows_out = row_features(cols_out, None)
    return (hidden_out, joint_gram(rows_in, rows_out, cols_in, cols_out))


def solution(mesh):
    return jax.shard_map(
        on_device,
        mesh=mesh,
        in_specs=(
            P("tok", "tp"),
            P(),
            P(None, "tp"),
            P(None, "tp"),
            P(None, "tp"),
            P("tp", None),
            P(),
        ),
        out_specs=(P("tok", "tp"), P(None, "tok", None, "tp")),
        check_vma=False,
    )
```

```python
import functools
import math

import jax
import jax.numpy as jnp
from jax import lax
from jax.experimental import pallas as pl
from jax.experimental.pallas import tpu as pltpu
from jax.sharding import PartitionSpec as P

HS = 128
epsilon = 1e-05
rope_base = 500000.0
VMEM_LIMIT = 60 * 1024 * 1024


def rotate(vectors, positions):
    half_dim = vectors.shape[-1] // 2
    inv_freq = rope_base ** (-(jnp.arange(half_dim, dtype=jnp.float32) * 2.0) / vectors.shape[-1])
    angles = positions.astype(jnp.float32)[:, None] * inv_freq[None, :]
    cosine = jnp.cos(angles)[:, None, :]
    sine_part = jnp.sin(angles)[:, None, :]
    first_half = vectors[..., :half_dim]
    second_half = vectors[..., half_dim:]
    return jnp.concatenate(
        [
            first_half * cosine - second_half * sine_part,
            second_half * cosine + first_half * sine_part,
        ],
        axis=-1,
    )


def attend_kernel(groups, block, bounds, q_ref, k_ref, v_ref, lo_ref, out_ref, s_ref, m_ref, l_ref, acc_ref):
    rows = q_ref.shape[0]
    first_row = bounds[0]
    scale = HS ** (-0.5) * math.log2(math.e)
    start = bounds[1] // block
    stop = (first_row + rows + block - 1) // block
    lanes = 128
    m_ref[...] = jnp.full_like(m_ref, -jnp.inf)
    l_ref[...] = jnp.zeros_like(l_ref)
    acc_ref[...] = jnp.zeros_like(acc_ref)

    @pl.loop(start, stop)
    def _(step):
        first_key = pl.multiple_of(step * block, block)
        keys = k_ref[pl.ds(first_key, block), :]
        key_pos = first_key + lax.broadcasted_iota(jnp.int32, (rows, block), 1)
        query_pos = first_row + lax.broadcasted_iota(jnp.int32, (rows, block), 0)
        allowed = (key_pos >= lo_ref[:, :1]) & (key_pos <= query_pos)
        for head in range(groups):
            part = pl.ds(head * rows, rows)
            s = lax.dot_general(
                q_ref[:, head * HS:(head + 1) * HS], keys,
                (((1,), (1,)), ((), ())), preferred_element_type=jnp.float32,
            ) * scale
            s = jnp.where(allowed, s, -jnp.inf)
            s_ref[step, part, :] = s
            top = m_ref[part, :]
            for piece in range(block // lanes):
                top = jnp.maximum(top, s[:, piece * lanes:(piece + 1) * lanes])
            m_ref[part, :] = top

    m_ref[...] = jnp.broadcast_to(jnp.max(m_ref[...], axis=-1, keepdims=True), m_ref.shape)

    @pl.loop(start, stop)
    def _(step):
        first_key = pl.multiple_of(step * block, block)
        values = v_ref[pl.ds(first_key, block), :]
        for head in range(groups):
            part = pl.ds(head * rows, rows)
            weights = jnp.exp2(s_ref[step, part, :] - m_ref[part, :1])
            total = l_ref[part, :]
            for piece in range(block // lanes):
                total = total + weights[:, piece * lanes:(piece + 1) * lanes]
            l_ref[part, :] = total
            acc_ref[part, :] += jnp.dot(
                weights.astype(jnp.bfloat16), values, preferred_element_type=jnp.float32
            )

    for head in range(groups):
        part = pl.ds(head * rows, rows)
        weight_sum = jnp.sum(l_ref[part, :], axis=-1, keepdims=True)
        out_ref[:, head * HS:(head + 1) * HS] = (acc_ref[part, :] / weight_sum).astype(out_ref.dtype)


def attend(queries, kv_rows, lo, bounds, kv_heads):
    rows, width = queries.shape
    all_rows = kv_rows.shape[1]
    groups = width // (kv_heads * HS)
    block = min(512, all_rows)
    wide = groups * HS
    return pl.pallas_call(
        functools.partial(attend_kernel, groups, block),
        out_shape=jax.ShapeDtypeStruct((rows, width), jnp.bfloat16),
        grid_spec=pltpu.PrefetchScalarGridSpec(
            num_scalar_prefetch=1,
            grid=(kv_heads,),
            in_specs=[
                pl.BlockSpec((rows, wide), lambda g, b: (0, g)),
                pl.BlockSpec((None, all_rows, HS), lambda g, b: (0, 0, g)),
                pl.BlockSpec((None, all_rows, HS), lambda g, b: (1, 0, g)),
                pl.BlockSpec((rows, 128), lambda g, b: (0, 0)),
            ],
            out_specs=pl.BlockSpec((rows, wide), lambda g, b: (0, g)),
            scratch_shapes=[
                pltpu.VMEM((all_rows // block, groups * rows, block), jnp.float32),
                pltpu.VMEM((groups * rows, 128), jnp.float32),
                pltpu.VMEM((groups * rows, 128), jnp.float32),
                pltpu.VMEM((groups * rows, HS), jnp.float32),
            ],
        ),
        compiler_params=pltpu.CompilerParams(
            dimension_semantics=("arbitrary",), vmem_limit_bytes=VMEM_LIMIT
        ),
        cost_estimate=pl.CostEstimate(
            flops=4 * rows * all_rows * width,
            bytes_accessed=2 * all_rows * kv_heads * HS * 2 + 4 * rows * width,
            transcendentals=rows * all_rows * width // HS,
        ),
        name="attend",
    )(bounds, queries, kv_rows, kv_rows, lo)


def gram_kernel(strips, rin_ref, rout_ref, low_ref, high_ref, cout_ref, out_ref, rt_ref, mean_ref):
    all_rows, row_width = rin_ref.shape

    @pl.when(pl.program_id(0) == 0)
    def _():
        ones = jnp.ones((all_rows, 128), jnp.bfloat16)
        for source, ref in enumerate((rin_ref, rout_ref)):
            part = pl.ds(source * row_width, row_width)
            rt_ref[part, :] = ref[...].T
            mean_ref[part, :] = (
                jnp.dot(rt_ref[part, :], ones, preferred_element_type=jnp.float32) / all_rows
            )

    ones = jnp.ones((8, all_rows), jnp.bfloat16)

    def block(source, ref):
        cols = ref[...]
        col_mean = jnp.dot(ones, cols, preferred_element_type=jnp.float32)[:1] / all_rows
        gram = jnp.dot(rt_ref[...], cols, preferred_element_type=jnp.float32)
        cov = gram / all_rows - mean_ref[:, :1] * col_mean
        for row_source in range(2):
            out_ref[row_source, :, source, :] = cov[row_source * row_width:(row_source + 1) * row_width]

    @pl.when(pl.program_id(0) < strips)
    def _():
        block(0, low_ref)

    @pl.when(pl.program_id(0) >= strips)
    def _():
        block(0, high_ref)

    block(1, cout_ref)


def joint_gram(rin, rout, cin, cout):
    all_rows, row_width = rin.shape
    half = cout.shape[2]
    col_width = 2 * half
    tile = min(256, half)
    strips = half // tile
    whole = pl.BlockSpec((all_rows, row_width), lambda j: (0, 0), pipeline_mode=pl.Buffered(1))
    strip = pl.BlockSpec((None, all_rows, tile), lambda j: (j // strips, 0, j % strips))
    low = pl.BlockSpec((all_rows, tile), lambda j: (0, jnp.minimum(j, strips - 1)))
    high = pl.BlockSpec((all_rows, tile), lambda j: (0, jnp.maximum(j - strips, 0)))
    return pl.pallas_call(
        functools.partial(gram_kernel, strips),
        out_shape=jax.ShapeDtypeStruct((2, row_width, 2, col_width), jnp.float32),
        grid=(col_width // tile,),
        in_specs=[whole, whole, low, high, strip],
        out_specs=pl.BlockSpec((2, row_width, 2, tile), lambda j: (0, 0, 0, j)),
        scratch_shapes=[
            pltpu.VMEM((2 * row_width, all_rows), jnp.bfloat16),
            pltpu.VMEM((2 * row_width, 128), jnp.float32),
        ],
        compiler_params=pltpu.CompilerParams(
            dimension_semantics=("arbitrary",), vmem_limit_bytes=VMEM_LIMIT
        ),
        cost_estimate=pl.CostEstimate(
            flops=8 * all_rows * row_width * col_width,
            bytes_accessed=4 * all_rows * (row_width + col_width) + 16 * row_width * col_width,
            transcendentals=0,
        ),
        name="joint_gram",
    )(rin, rout, *cin, cout)


def both_sides(block):
    if lax.axis_size("tp") != 2:
        return lax.all_gather(block, "tp", axis=1, tiled=True)
    other = lax.ppermute(block, "tp", ((0, 1), (1, 0)))
    first = lax.axis_index("tp") == 0
    return jnp.concatenate([jnp.where(first, block, other), jnp.where(first, other, block)], axis=1)


def ring_kernel(chips, share, x_ref, *refs):
    if share:
        out_ref, side_ref, send, recv, psend, precv, local, ssend, srecv = refs
    else:
        out_ref, send, recv, psend, precv, local = refs
    mesh_id = pl.DeviceIdType.MESH
    rows = x_ref.shape[1]
    me, tp = lax.axis_index("tok"), lax.axis_index("tp")
    count = 2 * chips
    core, chip = me % 2, me // 2
    depth = chips // 2
    spot = jnp.where(chip % 2 == 0, chip // 2, chips - 1 - chip // 2)

    def device(place):
        place = (place + 2 * chips) % chips
        return jnp.where(place < depth, place * 4, (chips - 1 - place) * 4 + 2) + core

    partner = me + 1 - 2 * core
    ways = (device(spot + 1), device(spot - 1))
    barrier = pltpu.get_barrier_semaphore()
    for peer in (*ways, partner):
        pl.semaphore_signal(barrier, inc=1, device_id={"tok": peer}, device_id_type=mesh_id)
    if share:
        pl.semaphore_signal(barrier, inc=1, device_id={"tp": 1 - tp}, device_id_type=mesh_id)
    pl.semaphore_wait(barrier, 4 if share else 3)

    def block(way, origin):
        return out_ref.at[way, pl.ds(pl.multiple_of(origin * rows, rows), rows), :]

    pending = []

    def step_copies(step, way):
        origin = device(spot - step if way == 0 else spot + step)
        source = x_ref.at[way] if step == 0 else block(way, origin)
        ring = None
        if step < chips - 1:
            ring = pltpu.make_async_remote_copy(
                src_ref=source, dst_ref=block(way, origin), send_sem=send.at[way, step],
                recv_sem=recv.at[way, step], device_id={"tok": ways[way]}, device_id_type=mesh_id,
            )
            ring.start()
        beside = pltpu.make_async_remote_copy(
            src_ref=source, dst_ref=block(way, origin), send_sem=psend.at[way, step],
            recv_sem=precv.at[way, step], device_id={"tok": partner}, device_id_type=mesh_id,
        )
        beside.start()
        pending.append((ring, beside))
        return ring

    rings = [step_copies(0, way) for way in range(2)]
    own = [pltpu.make_async_copy(x_ref.at[way], block(way, me), local.at[way]) for way in range(2)]
    for copy in own:
        copy.start()
    if share:
        width = side_ref.shape[1]
        half = x_ref.shape[2]
        owner = me // (count // 2)
        my_way = me * width % (2 * half) // half
        features = pl.ds(pl.multiple_of(me * width % half, width), width)

    def side_copy(step, way, kind):
        origin = device(spot - step if way == 0 else spot + step)
        origin = origin + kind * (1 - 2 * core)
        source = x_ref.at[way, :, features]
        if step > 0 or kind > 0:
            source = out_ref.at[way, pl.ds(pl.multiple_of(origin * rows, rows), rows), features]
        return pltpu.make_async_remote_copy(
            src_ref=source,
            dst_ref=side_ref.at[pl.ds(pl.multiple_of(origin * rows, rows), rows), :],
            send_sem=ssend.at[kind, step], recv_sem=srecv.at[kind, step],
            device_id={"tp": 1 - tp}, device_id_type=mesh_id,
        )

    def each_side(act, step, way, kind, holder):
        if share:
            @pl.when((my_way == way) & ((owner == tp) == holder))
            def _():
                act(side_copy(step, way, kind))

    def start(copy):
        copy.start()

    for way in range(2):
        each_side(start, 0, way, 0, True)
    for step in range(1, chips):
        for way in range(2):
            rings[way].wait_recv()
            rings[way] = step_copies(step, way)
            each_side(start, step, way, 0, True)
            pending[2 * (step - 1) + way][1].wait_recv()
            each_side(start, step - 1, way, 1, True)
    for way in range(2):
        pending[2 * (chips - 1) + way][1].wait_recv()
        each_side(start, chips - 1, way, 1, True)
    for ring, beside in pending:
        if ring is not None:
            ring.wait_send()
        beside.wait_send()
    for copy in own:
        copy.wait()
    for step in range(chips):
        for way in range(2):
            for kind in range(2):
                each_side(lambda copy: copy.wait_send(), step, way, kind, True)
                each_side(lambda copy: copy.wait_recv(), step, way, kind, False)


def ring_gather(halves, share, call_id):
    _, rows, width = halves.shape
    count = lax.axis_size("tok")
    chips = count // 2
    out_shape = [jax.ShapeDtypeStruct((2, rows * count, width), halves.dtype)]
    dma = pltpu.SemaphoreType.DMA
    scratch = [dma((2, chips))] * 4 + [dma((2,))]
    if share:
        out_shape.append(jax.ShapeDtypeStruct((rows * count, 4 * width // count), halves.dtype))
        scratch += [dma((2, chips))] * 2
    return pl.pallas_call(
        functools.partial(ring_kernel, chips, share),
        out_shape=out_shape,
        in_specs=[pl.BlockSpec(memory_space=pltpu.VMEM)],
        out_specs=[pl.BlockSpec(memory_space=pl.ANY)] * len(out_shape),
        scratch_shapes=scratch,
        compiler_params=pltpu.CompilerParams(
            collective_id=call_id, has_side_effects=True, vmem_limit_bytes=VMEM_LIMIT
        ),
        cost_estimate=pl.CostEstimate(
            flops=40_000_000_000, bytes_accessed=2 * halves.size * count * 2, transcendentals=0
        ),
        name="ring_share" if share else "ring",
    )(halves)


def row_features(columns, arrived):
    _, all_rows, half = columns.shape
    row_width = 2 * half * lax.axis_size("tp") // lax.axis_size("tok")
    first = lax.axis_index("tok") * row_width
    offset, owner = first % (2 * half), first // (2 * half)
    mine = lax.dynamic_slice(columns, (offset // half, 0, offset % half), (1, all_rows, row_width))[0]
    owned = lax.axis_index("tp") == owner
    if arrived is None:
        return lax.psum(jnp.where(owned, mine, jnp.zeros_like(mine)), "tp")
    return jnp.where(owned, mine, arrived)


def on_device(hidden_in, norm_gain, w_query, w_key, w_value, w_out, doc_ids):
    tok_rows, col_width = hidden_in.shape
    tok_count = lax.axis_size("tok")
    tp_count = lax.axis_size("tp")
    tok_index = lax.axis_index("tok")
    all_rows = tok_rows * tok_count
    full_in = both_sides(hidden_in)
    widened = full_in.astype(jnp.float32)
    factor = lax.rsqrt(jnp.mean(widened * widened, axis=1, keepdims=True) + epsilon)
    normed = (widened * factor * norm_gain[None, :]).astype(jnp.bfloat16)
    kv_heads = w_key.shape[1] // HS
    groups = w_query.shape[1] // w_key.shape[1]
    first_row = tok_index * tok_rows
    positions = first_row + jnp.arange(tok_rows, dtype=jnp.int32)
    key_local = rotate(
        jnp.dot(normed, w_key, preferred_element_type=jnp.float32).reshape(tok_rows, kv_heads, HS),
        positions % all_rows,
    )
    key_local = key_local.astype(jnp.bfloat16).reshape(tok_rows, kv_heads * HS)
    value_local = jnp.dot(normed, w_value, preferred_element_type=jnp.float32).astype(jnp.bfloat16)
    (kv_rows,) = ring_gather(jnp.stack([key_local, value_local]), False, 0)
    early, late = hidden_in[:, : col_width // 2], hidden_in[:, col_width // 2 :]
    late, kv_rows = lax.optimization_barrier((late, kv_rows))
    cols_in = [lax.all_gather(part, "tok", axis=0, tiled=True) for part in (early, late)]
    rows_in = lax.all_to_all(full_in, "tok", 1, 0, tiled=True)
    queries = rotate(
        jnp.dot(normed, w_query, preferred_element_type=jnp.float32).reshape(
            tok_rows, kv_heads * groups, HS
        ),
        positions % all_rows,
    )
    queries = queries.astype(jnp.bfloat16).reshape(tok_rows, kv_heads * groups * HS)
    query_doc = lax.dynamic_slice_in_dim(doc_ids, first_row, tok_rows, 0)
    lo = jnp.sum((doc_ids[None, :] < query_doc[:, None]).astype(jnp.int32), axis=1)
    bounds = jnp.stack([first_row.astype(jnp.int32), lo[0]])
    attended = attend(queries, kv_rows, jnp.broadcast_to(lo[:, None], (tok_rows, 128)), bounds, kv_heads)
    partial_out = jnp.dot(attended, w_out, preferred_element_type=jnp.float32)
    if tp_count == 2:
        first = lax.axis_index("tp") == 0
        low, high = partial_out[:, :col_width], partial_out[:, col_width:]
        sent = jnp.where(first, high, low).astype(jnp.bfloat16)
        arrived = lax.ppermute(sent, "tp", ((0, 1), (1, 0)))
        summed = jnp.where(first, low, high) + arrived.astype(jnp.float32)
    else:
        summed = lax.psum_scatter(partial_out, "tp", scatter_dimension=1, tiled=True)
    hidden_out = (hidden_in.astype(jnp.float32) + summed).astype(jnp.bfloat16)
    halves = jnp.stack([hidden_out[:, : col_width // 2], hidden_out[:, col_width // 2 :]])
    if tp_count == 2:
        cols_out, arrived_rows = ring_gather(halves, True, 1)
        rows_out = row_features(cols_out, arrived_rows)
    else:
        (cols_out,) = ring_gather(halves, False, 1)
        rows_out = row_features(cols_out, None)
    return (hidden_out, joint_gram(rows_in, rows_out, cols_in, cols_out))


def solution(mesh):
    return jax.shard_map(
        on_device,
        mesh=mesh,
        in_specs=(
            P("tok", "tp"),
            P(),
            P(None, "tp"),
            P(None, "tp"),
            P(None, "tp"),
            P("tp", None),
            P(),
        ),
        out_specs=(P("tok", "tp"), P(None, "tok", None, "tp")),
        check_vma=False,
    )
```
